32 devices in a mesh: dom: 16 (over z, y, x), ens: 2 (over core).
Axes of the slice: x: 2, y: 2, z: 4, core: 2. Of those that a mesh axis runs over, the one named last changes fastest.
Arguments:
- alpha: float32 [20, 4, 128, 512], P('ens', None, 'dom'), may hold values from -2.5 to 2.5
- perturb: bfloat16 [20, 4, 128, 512], P('ens', None, 'dom'), may hold values from -6 to 6
- static_ctl: float32 [4, 128, 512], P(None, 'dom'), may hold values from -6 to 6
- sigma: float32 [4, 128, 512], P(None, 'dom'), may hold values from 0.3 to 3
- class_index: int32 [4, 128, 512], P(None, 'dom'), may hold values from 0 to 7
- class_kappa: float32 [8], replicated, may hold values from 0.02 to 0.24
- obs_cell: int32 [32768], P('dom'), may hold values from 0 to 16383
- obs_value: float32 [32768], P('dom'), may hold values from -6 to 6
- obs_weight: float32 [32768], P('dom'), may hold values from 2 to 20
Outputs:
- grad_alpha: float32 [20, 4, 128, 512], P('ens', None, 'dom')
- grad_static: float32 [4, 128, 512], P(None, 'dom')
The draws below stay inside these ranges and needn't reach their ends.
Inputs may be any that keep to these rules, and one draw needn't show every extreme that they name: obs_cell[k] is a cell, in the order level, column, row, of the block of 8 columns that starts at column (k // 2048) * 8.
All inputs are finite; a program needn't handle non-finite values.
Results may differ from the reference program's by a relative error of at most 0.0005.
Values sent between devices are 32-bit elements; how exact they have to be, the bound alone decides.
A program may use at most 64 MiB of HBM per device.

```python
import math
import jax
import jax.numpy as jnp
from jax import lax

CX = 8
CY = 512
LEV = 4
NOBS_DEV = 2048
PASSES = 4
NCLASS = 8
MEMBERS = 20
NX = 128
NOBS = 32768


def plant(array, own_key, smallest, top_value):
    longest = array.shape.index(max(array.shape))
    spots = []
    for shift in (0, 1):
        where = [jax.random.randint(jax.random.fold_in(own_key, axis), (), 0, length) for axis, length in enumerate(array.shape)]
        where[longest] = (where[longest] + shift) % array.shape[longest]
        spots.append(tuple(where))
    return array.at[spots[0]].set(smallest).at[spots[1]].set(top_value)


def block_scale(stream_key, extent, pieces, smallest, high):
    factor_of, own = 1.0, jax.random.fold_in(stream_key, 6)
    for axis_at, shards_of in pieces:
        heights = jnp.exp(jax.random.uniform(jax.random.fold_in(own, axis_at), (shards_of,), jnp.float32, smallest / len(pieces), high / len(pieces)))
        factor_of = factor_of * jnp.repeat(heights, extent[axis_at] // shards_of).reshape([-1 if axis == axis_at else 1 for axis in range(len(extent))])
    return factor_of


def gaussian(key, extent, width, reach, split=(), held_as=jnp.bfloat16):
    result = jax.random.normal(key, extent, jnp.float32) * width
    if len(split) > 0:
        result = block_scale(key, extent, split, -0.22, 0.18) * result
    return jnp.clip(result, min=-reach, max=reach).astype(held_as)


def setup_inputs(seed: int = 0) -> dict:
    splits = jax.random.split(jax.random.key(seed), 10)
    return {
        "alpha": gaussian(splits[0], (MEMBERS, LEV, NX, CY), 0.3, 2.5, ((0, 2), (2, 16)), jnp.float32),
        "perturb": gaussian(splits[1], (MEMBERS, LEV, NX, CY), 1.0, 6.0, ((0, 2), (2, 16))),
        "static_ctl": gaussian(splits[2], (LEV, NX, CY), 1.0, 6.0, ((1, 16),), jnp.float32),
        "sigma": jnp.clip(jnp.exp(math.log(3.0) - 2.3025851 * jax.random.uniform(splits[3], (LEV, NX, CY), jnp.float32) ** block_scale(splits[3], (LEV, NX, CY), ((1, 16),), -0.2, 0.2)), 0.3, 3.0),
        "class_index": plant(jax.random.randint(splits[4], (LEV, NX, CY), 0, NCLASS), jax.random.fold_in(splits[4], 1), 0, NCLASS - 1).astype(jnp.int32),
        "class_kappa": jnp.clip(jax.random.uniform(splits[5], (NCLASS,), jnp.float32, 0.02, 0.24), 0.02, 0.24),
        "obs_cell": plant(jax.random.randint(splits[6], (NOBS,), 0, LEV * CX * CY), jax.random.fold_in(splits[6], 1), 0, (LEV * CX * CY) - 1).astype(jnp.int32),
        "obs_value": gaussian(splits[7], (NOBS,), 1.0, 6.0, ((0, 16),), jnp.float32),
        "obs_weight": jnp.clip(jnp.exp(math.log(20.0) - 2.3025851 * jax.random.uniform(splits[8], (NOBS,), jnp.float32) ** block_scale(splits[8], (NOBS,), ((0, 16),), -0.2, 0.2)), 2.0, 20.0),
    }


def one_pass(field, face_x, face_y):
    flux_x = face_x * (jnp.roll(field, -1, axis=-2) - field)
    flux_y = face_y * (field[..., 1:] - field[..., :-1])
    padded = jnp.pad(flux_y, [(0, 0)] * (flux_y.ndim - 1) + [(1, 1)])
    return field + (flux_x - jnp.roll(flux_x, 1, axis=-2)) + (padded[..., 1:] - padded[..., :-1])

def reference(alpha, perturb, static_ctl, sigma, class_index, class_kappa, obs_cell, obs_value, obs_weight):
    coeff = jnp.take(class_kappa, class_index)
    face_x = 0.5 * (coeff + jnp.roll(coeff, -1, axis=1))
    face_y = 0.5 * (coeff[..., :-1] + coeff[..., 1:])

    def diffuse(field):
        for index in range(PASSES):
            field = one_pass(field, face_x, face_y)
        return field
    scale = 1.0 / math.sqrt(MEMBERS - 1)

    def accumulate(total, member):
        return (total + member[1].astype(jnp.float32) * diffuse(member[0]), None)
    increment, unused = lax.scan(accumulate, jnp.zeros(static_ctl.shape, jnp.float32), (alpha, perturb))
    state = sigma * static_ctl + scale * increment
    plane = CX * CY
    block = (jnp.arange(obs_cell.shape[0], dtype=jnp.int32) // NOBS_DEV).astype(jnp.int32)
    level_index = obs_cell // plane
    remainder = obs_cell % plane
    column = block * CX + remainder // CY
    row_index = remainder % CY
    values = state[level_index, column, row_index]
    weighted = obs_weight * (values - obs_value)
    adjoint = jnp.zeros(static_ctl.shape, jnp.float32).at[level_index, column, row_index].add(weighted)
    grad_static = static_ctl + sigma * adjoint

    def member_grad(member):
        return member[0] + scale * diffuse(member[1].astype(jnp.float32) * adjoint)
    grad_alpha = lax.map(member_grad, (alpha, perturb))
    return (grad_alpha, grad_static)
```

```python
import functools
import math

import jax
import jax.numpy as jnp
from jax import lax
from jax.experimental import pallas as pl
from jax.experimental.pallas import tpu as pltpu
from jax.sharding import PartitionSpec as P

PASSES = 4
MESH = pl.DeviceIdType.MESH
LANES = 128
PIECES = 3
CHUNKS = 2


def sublane(shape):
    return lax.broadcasted_iota(jnp.int32, shape, len(shape) - 2)


def roll(x, shift, axis):
    return pltpu.roll(x, shift, axis % x.ndim)


def toward_right(own, halo):
    last = sublane(own.shape) == 7
    a, b = roll(own, 7, -2), roll(halo, 7, -2)
    return jnp.where(last, b, a), jnp.where(last, a, b)


def toward_left(own, halo):
    first = sublane(own.shape) == 0
    a, b = roll(own, 1, -2), roll(halo, 1, -2)
    return jnp.where(first, b, a), jnp.where(first, a, b)


def pack(a, b):
    top = sublane(a.shape) < 4
    return jnp.where(top, a, roll(b, 4, -2)), jnp.where(top, roll(a, 4, -2), b)


def faces(own, halo):
    right_own, right_halo = toward_right(own, halo)
    rows = own.shape[-1]
    inside = lax.broadcasted_iota(jnp.int32, own.shape, own.ndim - 1) < rows - 1
    zero = jnp.zeros_like(own)
    fx_own = 0.5 * (own + right_own)
    fx_halo = jnp.where(sublane(own.shape) == 3, zero, 0.5 * (halo + right_halo))
    fy_own = jnp.where(inside, 0.5 * (own + roll(own, rows - 1, -1)), zero)
    fy_halo = jnp.where(inside, 0.5 * (halo + roll(halo, rows - 1, -1)), zero)
    return fx_own, fx_halo, fy_own, fy_halo


def diffuse(own, halo, fx_own, fx_halo, fy_own, fy_halo):
    rows = own.shape[-1]
    for _ in range(PASSES):
        right_own, right_halo = toward_right(own, halo)
        flux_own = fx_own * (right_own - own)
        flux_halo = fx_halo * (right_halo - halo)
        left_own, left_halo = toward_left(flux_own, flux_halo)
        up_own = fy_own * (roll(own, rows - 1, -1) - own)
        up_halo = fy_halo * (roll(halo, rows - 1, -1) - halo)
        own = own + (flux_own - left_own) + (up_own - roll(up_own, 1, -1))
        halo = halo + (flux_halo - left_halo) + (up_halo - roll(up_halo, 1, -1))
    return own, halo


def split3(x):
    out = []
    for _ in range(PIECES):
        piece = x.astype(jnp.bfloat16)
        out.append(piece.astype(jnp.float32))
        x = x - out[-1]
    return out


def scatter(cell, weight, product, hot_hi, hot_lo):
    groups = cell.shape[0]
    spot = lax.broadcasted_iota(jnp.int32, (LANES, LANES), 0)
    for g in range(groups):
        c = cell[g : g + 1, :]
        hi = (c // 4096) * 32 + ((c // 128) % 4) * 8 + (c // 512) % 8
        lo = c % 128
        lanes = slice(g * LANES, (g + 1) * LANES)
        hot_hi[:, lanes] = (spot == hi).astype(jnp.float32).astype(jnp.bfloat16)
        here = spot == lo
        values = split3(weight[g : g + 1, :]) + split3(product[g : g + 1, :])
        for i, value in enumerate(values):
            hot_lo[i * LANES : (i + 1) * LANES, lanes] = jnp.where(here, value, 0.0).astype(
                jnp.bfloat16
            )


def exchange(
    n_dom, n_ens, scale,
    kappa, alpha, perturb, static, sigma, index, obs_cell, obs_value, obs_weight,
    adj_out, ph_out, fx_out, fy_out,
    c_send, c_recv, p_send, p_recv, e_send, e_recv, a_send, a_recv, total,
    tail, weights, hot_hi, hot_lo,
    c_ss, c_rs, p_ss, p_rs, e_ss, e_rs, a_ss, a_rs, t_ss, t_rs,
):
    me, ens = lax.axis_index("dom"), lax.axis_index("ens")
    right, left = lax.rem(me + 1, n_dom), lax.rem(me + n_dom - 1, n_dom)
    members, levels = alpha.shape[0], alpha.shape[1]
    rows = alpha.shape[3]

    barrier = pltpu.get_barrier_semaphore()
    for side in (left, right):
        pl.semaphore_signal(barrier, inc=1, device_id=(side, ens), device_id_type=MESH)
    for r in range(1, n_ens):
        pl.semaphore_signal(
            barrier, inc=1, device_id=(me, lax.rem(ens + r, n_ens)), device_id_type=MESH
        )

    def send(src, dst, ss, rs, side):
        copy = pltpu.make_async_remote_copy(
            src_ref=src, dst_ref=dst, send_sem=ss, recv_sem=rs,
            device_id=(side, ens), device_id_type=MESH,
        )
        copy.start()
        return copy

    cls = index[...]
    coeff = jnp.zeros(cls.shape, jnp.float32)
    for number in range(kappa.shape[0]):
        coeff = jnp.where(cls == number, kappa[number], coeff)
    for pair in range(levels // 2):
        low, high = pack(coeff[2 * pair], coeff[2 * pair + 1])
        c_send[0, pair] = low
        c_send[1, pair] = high
    pl.semaphore_wait(barrier, 2 + n_ens - 1)
    coeff_copies = [
        send(c_send.at[s], c_recv.at[s], c_ss.at[s], c_rs.at[s], side)
        for s, side in ((0, left), (1, right))
    ]
    part = members // CHUNKS
    halo_copies = []
    for chunk in range(CHUNKS):
        def fill(m, carry):
            for pair in range(levels // 2):
                a = perturb[m, 2 * pair].astype(jnp.float32)
                b = perturb[m, 2 * pair + 1].astype(jnp.float32)
                low, high = pack(a, b)
                p_send[0, m, pair] = low
                p_send[1, m, pair] = high
            return carry

        lax.fori_loop(chunk * part, (chunk + 1) * part, fill, 0)
        span = pl.ds(chunk * part, part)
        halo_copies.append([
            send(p_send.at[s, span], p_recv.at[s, span],
                 p_ss.at[s, chunk], p_rs.at[s, chunk], side)
            for s, side in ((0, left), (1, right))
        ])

    scatter(
        obs_cell[...], obs_weight[...], obs_weight[...] * obs_value[...], hot_hi, hot_lo
    )
    sums = lax.dot_general(
        hot_hi[...], hot_lo[...], (((1,), (1,)), ((), ())), preferred_element_type=jnp.float32
    )
    for which in range(2):
        whole = sums[:, which * PIECES * LANES : (which * PIECES + 1) * LANES]
        for i in range(1, PIECES):
            at = (which * PIECES + i) * LANES
            whole = whole + sums[:, at : at + LANES]
        for level in range(levels):
            for block in range(rows // LANES):
                at = (level * (rows // LANES) + block) * 8
                weights[which, level, :, block * LANES : (block + 1) * LANES] = whole[at : at + 8]

    for copy in coeff_copies:
        copy.wait()
    for pair in range(levels // 2):
        for i in range(2):
            level = 2 * pair + i
            halo = halo_tile(c_recv[0, pair], c_recv[1, pair], i)
            f = faces(coeff[level], halo)
            fx_out[0, level], fx_out[1, level], fy_out[0, level], fy_out[1, level] = f

    for level in range(levels):
        f = (fx_out[0, level], fx_out[1, level], fy_out[0, level], fy_out[1, level])

        def smooth(m, acc):
            own, halo = diffuse(
                alpha[m, level], jnp.zeros((8, rows), jnp.float32), *f
            )
            tail[m, level] = halo
            return acc + perturb[m, level].astype(jnp.float32) * own

        total[0, level] = lax.fori_loop(
            0, members, smooth, jnp.zeros((8, rows), jnp.float32), unroll=2
        )

    edge = [jnp.zeros((8, rows), jnp.float32)] * levels
    for chunk in range(CHUNKS):
        for copy in halo_copies[chunk]:
            copy.wait()

        def gather(m, acc):
            out = []
            for level in range(levels):
                halo = halo_tile(p_recv[0, m, level // 2], p_recv[1, m, level // 2], level % 2)
                ph_out[m, level] = halo
                out.append(acc[level] + halo * tail[m, level])
            return tuple(out)

        edge = lax.fori_loop(chunk * part, (chunk + 1) * part, gather, tuple(edge))
    for pair in range(levels // 2):
        low, high = pack(edge[2 * pair], edge[2 * pair + 1])
        e_send[0, pair] = low
        e_send[1, pair] = high
    edge_copies = [
        send(e_send.at[s], e_recv.at[s], e_ss.at[s], e_rs.at[s], side)
        for s, side in ((0, right), (1, left))
    ]
    for copy in edge_copies:
        copy.wait()
    for level in range(levels):
        total[0, level] = total[0, level] + halo_tile(
            e_recv[0, level // 2], e_recv[1, level // 2], level % 2
        )
    sums_copies = []
    for r in range(1, n_ens):
        copy = pltpu.make_async_remote_copy(
            src_ref=total.at[0], dst_ref=total.at[r],
            send_sem=t_ss.at[r], recv_sem=t_rs.at[r],
            device_id=(me, lax.rem(ens + r, n_ens)), device_id_type=MESH,
        )
        copy.start()
        sums_copies.append(copy)
    for copy in sums_copies:
        copy.wait()
    increment = total[lax.rem(ens + n_ens, n_ens)]
    for j in range(1, n_ens):
        increment = increment + total[lax.rem(ens - j + n_ens, n_ens)]
    state = sigma[...] * static[...] + scale * increment
    adjoint = weights[0] * state - weights[1]
    adj_out[0] = adjoint
    for pair in range(levels // 2):
        low, high = pack(adjoint[2 * pair], adjoint[2 * pair + 1])
        a_send[0, pair] = low
        a_send[1, pair] = high
    adjoint_copies = [
        send(a_send.at[s], a_recv.at[s], a_ss.at[s], a_rs.at[s], side)
        for s, side in ((0, left), (1, right))
    ]
    for copy in adjoint_copies:
        copy.wait()
    for level in range(levels):
        adj_out[1, level] = halo_tile(a_recv[0, level // 2], a_recv[1, level // 2], level % 2)


def halo_tile(first, second, i):
    top = sublane(first.shape) < 4
    if i == 0:
        return jnp.where(top, first, roll(second, 4, -2))
    return jnp.where(top, roll(first, 4, -2), second)


def finish(scale, alpha, perturb, ph, adj, fx, fy, static, sigma, ga, gs):
    @pl.when(pl.program_id(0) == 0)
    def _():
        gs[...] = static[...] + sigma[...] * adj[0]

    for m in range(alpha.shape[0]):
        for level in range(alpha.shape[1]):
            own = perturb[m, level].astype(jnp.float32) * adj[0, level]
            halo = ph[m, level] * adj[1, level]
            own, halo = diffuse(
                own, halo, fx[0, level], fx[1, level], fy[0, level], fy[1, level]
            )
            ga[m, level] = alpha[m, level] + scale * own


def per_device(
    alpha, perturb, static_ctl, sigma, class_index, class_kappa, obs_cell, obs_value, obs_weight
):
    n_dom, n_ens = lax.axis_size("dom"), lax.axis_size("ens")
    local, levels, columns, rows = alpha.shape
    assert columns == 8 and levels == 4 and rows == 512
    scale = 1.0 / math.sqrt(local * n_ens - 1)
    groups = obs_cell.shape[0] // LANES
    f32 = jnp.float32
    tile = (levels, columns, rows)
    half = (2, levels // 2, columns, rows)
    vmem = pl.BlockSpec(memory_space=pltpu.VMEM)
    dma = pltpu.SemaphoreType.DMA
    adj, ph, fx, fy = pl.pallas_call(
        functools.partial(exchange, n_dom, n_ens, scale),
        out_shape=(
            jax.ShapeDtypeStruct((2,) + tile, f32),
            jax.ShapeDtypeStruct((local,) + tile, f32),
            jax.ShapeDtypeStruct((2,) + tile, f32),
            jax.ShapeDtypeStruct((2,) + tile, f32),
        ),
        in_specs=[pl.BlockSpec(memory_space=pltpu.SMEM)] + [vmem] * 8,
        out_specs=(vmem,) * 4,
        scratch_shapes=[
            pltpu.VMEM(half, f32),
            pltpu.VMEM(half, f32),
            pltpu.VMEM((2, local) + half[1:], f32),
            pltpu.VMEM((2, local) + half[1:], f32),
            pltpu.VMEM(half, f32),
            pltpu.VMEM(half, f32),
            pltpu.VMEM(half, f32),
            pltpu.VMEM(half, f32),
            pltpu.VMEM((n_ens,) + tile, f32),
            pltpu.VMEM((local,) + tile, f32),
            pltpu.VMEM((2,) + tile, f32),
            pltpu.VMEM((LANES, groups * LANES), jnp.bfloat16),
            pltpu.VMEM((2 * PIECES * LANES, groups * LANES), jnp.bfloat16),
            dma((2,)), dma((2,)),
            dma((2, CHUNKS)), dma((2, CHUNKS)),
            dma((2,)), dma((2,)),
            dma((2,)), dma((2,)),
            dma((n_ens,)), dma((n_ens,)),
        ],
        compiler_params=pltpu.CompilerParams(
            collective_id=0, has_side_effects=True, vmem_limit_bytes=40 * 2**20
        ),
        name="exchange",
    )(
        class_kappa, alpha, perturb, static_ctl, sigma, class_index,
        obs_cell.reshape(groups, LANES), obs_value.reshape(groups, LANES),
        obs_weight.reshape(groups, LANES),
    )
    block = 2
    moving = pl.BlockSpec((block,) + tile, lambda i: (i, 0, 0, 0))
    fixed = pl.BlockSpec((2,) + tile, lambda i: (0, 0, 0, 0))
    plain = pl.BlockSpec(tile, lambda i: (0, 0, 0))
    return pl.pallas_call(
        functools.partial(finish, scale),
        out_shape=(
            jax.ShapeDtypeStruct(alpha.shape, f32),
            jax.ShapeDtypeStruct(static_ctl.shape, f32),
        ),
        grid=(local // block,),
        in_specs=[moving, moving, moving, fixed, fixed, fixed, plain, plain],
        out_specs=(moving, plain),
        name="finish",
    )(alpha, perturb, ph, adj, fx, fy, static_ctl, sigma)


def solution(mesh):
    return jax.shard_map(
        per_device,
        mesh=mesh,
        in_specs=(
            P("ens", None, "dom", None),
            P("ens", None, "dom", None),
            P(None, "dom", None),
            P(None, "dom", None),
            P(None, "dom", None),
            P(),
            P("dom"),
            P("dom"),
            P("dom"),
        ),
        out_specs=(P("ens", None, "dom", None), P(None, "dom", None)),
        check_vma=False,
    )
```

```python
import functools
import math

import jax
import jax.numpy as jnp
from jax import lax
from jax.experimental import pallas as pl
from jax.experimental.pallas import tpu as pltpu
from jax.sharding import PartitionSpec as P

PASSES = 4
MESH = pl.DeviceIdType.MESH
LANES = 128
PIECES = 3
CHUNKS = 5
BATCH = 2


def sublane(shape):
    return lax.broadcasted_iota(jnp.int32, shape, len(shape) - 2)


def roll(x, shift, axis):
    return pltpu.roll(x, shift, axis % x.ndim)


def toward_right(own, halo):
    last = sublane(own.shape) == 7
    a, b = roll(own, 7, -2), roll(halo, 7, -2)
    return jnp.where(last, b, a), jnp.where(last, a, b)


def toward_left(own, halo):
    first = sublane(own.shape) == 0
    a, b = roll(own, 1, -2), roll(halo, 1, -2)
    return jnp.where(first, b, a), jnp.where(first, a, b)


def pack(a, b):
    top = sublane(a.shape) < 4
    return jnp.where(top, a, roll(b, 4, -2)), jnp.where(top, roll(a, 4, -2), b)


def faces(own, halo):
    right_own, right_halo = toward_right(own, halo)
    rows = own.shape[-1]
    inside = lax.broadcasted_iota(jnp.int32, own.shape, own.ndim - 1) < rows - 1
    zero = jnp.zeros_like(own)
    fx_own = 0.5 * (own + right_own)
    fx_halo = jnp.where(sublane(own.shape) == 3, zero, 0.5 * (halo + right_halo))
    fy_own = jnp.where(inside, 0.5 * (own + roll(own, rows - 1, -1)), zero)
    fy_halo = jnp.where(inside, 0.5 * (halo + roll(halo, rows - 1, -1)), zero)
    return fx_own, fx_halo, fy_own, fy_halo


def diffuse(own, halo, fx_own, fx_halo, fy_own, fy_halo):
    rows = own.shape[-1]
    for _ in range(PASSES):
        right_own, right_halo = toward_right(own, halo)
        flux_own = fx_own * (right_own - own)
        flux_halo = fx_halo * (right_halo - halo)
        left_own, left_halo = toward_left(flux_own, flux_halo)
        up_own = fy_own * (roll(own, rows - 1, -1) - own)
        up_halo = fy_halo * (roll(halo, rows - 1, -1) - halo)
        own = own + (flux_own - left_own) + (up_own - roll(up_own, 1, -1))
        halo = halo + (flux_halo - left_halo) + (up_halo - roll(up_halo, 1, -1))
    return own, halo


def split3(x):
    out = []
    for _ in range(PIECES):
        piece = x.astype(jnp.bfloat16)
        out.append(piece.astype(jnp.float32))
        x = x - out[-1]
    return out


def scatter(cell, weight, product, hot_hi, hot_lo):
    groups = cell.shape[0]
    spot = lax.broadcasted_iota(jnp.int32, (LANES, LANES), 0)
    for g in range(groups):
        c = cell[g : g + 1, :]
        hi = (c // 4096) * 32 + ((c // 128) % 4) * 8 + (c // 512) % 8
        lo = c % 128
        lanes = slice(g * LANES, (g + 1) * LANES)
        hot_hi[:, lanes] = (spot == hi).astype(jnp.float32).astype(jnp.bfloat16)
        here = spot == lo
        values = split3(weight[g : g + 1, :]) + split3(product[g : g + 1, :])
        for i, value in enumerate(values):
            hot_lo[i * LANES : (i + 1) * LANES, lanes] = jnp.where(here, value, 0.0).astype(
                jnp.bfloat16
            )


def exchange(
    n_dom, n_ens, scale,
    kappa_in, alpha_in, perturb_in, static_in, sigma_in, index_in, cell_in, value_in, weight_in,
    ga, gs,
    adj_out, ph_out, fx_out, fy_out, alpha, perturb, gs_out, kappa, static, sigma, index, obs_cell, obs_value, obs_weight,
    c_send, c_recv, p_send, p_recv, e_send, e_recv, a_send, a_recv, total,
    tail, weights, hot_hi, hot_lo,
    in_sem, pin_sem, ga_sem, gs_sem, c_ss, c_rs, p_ss, p_rs, e_ss, e_rs, a_ss, a_rs, t_ss, t_rs,
):
    me, ens = lax.axis_index("dom"), lax.axis_index("ens")
    right, left = lax.rem(me + 1, n_dom), lax.rem(me + n_dom - 1, n_dom)
    members, levels = alpha.shape[0], alpha.shape[1]
    rows = alpha.shape[3]

    part = members // CHUNKS
    loads = []
    for i, (src, dst) in enumerate((
        (kappa_in, kappa), (index_in, index), (cell_in, obs_cell), (value_in, obs_value),
        (weight_in, obs_weight), (static_in, static), (sigma_in, sigma), (alpha_in, alpha),
    )):
        loads.append(pltpu.make_async_copy(src, dst, in_sem.at[i]))
    perturb_loads = [
        pltpu.make_async_copy(
            perturb_in.at[pl.ds(c * part, part)], perturb.at[pl.ds(c * part, part)], pin_sem.at[c]
        )
        for c in range(CHUNKS)
    ]
    for copy in loads[:2] + perturb_loads + loads[2:]:
        copy.start()

    barrier = pltpu.get_barrier_semaphore()
    for side in (left, right):
        pl.semaphore_signal(barrier, inc=1, device_id=(side, ens), device_id_type=MESH)
    for r in range(1, n_ens):
        pl.semaphore_signal(
            barrier, inc=1, device_id=(me, lax.rem(ens + r, n_ens)), device_id_type=MESH
        )

    def send(src, dst, ss, rs, side):
        copy = pltpu.make_async_remote_copy(
            src_ref=src, dst_ref=dst, send_sem=ss, recv_sem=rs,
            device_id=(side, ens), device_id_type=MESH,
        )
        copy.start()
        return copy

    loads[0].wait()
    loads[1].wait()
    cls = index[...]
    coeff = jnp.zeros(cls.shape, jnp.float32)
    for number in range(kappa.shape[0]):
        coeff = jnp.where(cls == number, kappa[number], coeff)
    for pair in range(levels // 2):
        low, high = pack(coeff[2 * pair], coeff[2 * pair + 1])
        c_send[0, pair] = low
        c_send[1, pair] = high
    pl.semaphore_wait(barrier, 2 + n_ens - 1)
    coeff_copies = [
        send(c_send.at[s], c_recv.at[s], c_ss.at[s], c_rs.at[s], side)
        for s, side in ((0, left), (1, right))
    ]
    halo_copies = []
    for chunk in range(CHUNKS):
        perturb_loads[chunk].wait()

        def fill(m, carry):
            for pair in range(levels // 2):
                a = perturb[m, 2 * pair].astype(jnp.float32)
                b = perturb[m, 2 * pair + 1].astype(jnp.float32)
                low, high = pack(a, b)
                p_send[0, m, pair] = low
                p_send[1, m, pair] = high
            return carry

        lax.fori_loop(chunk * part, (chunk + 1) * part, fill, 0)
        span = pl.ds(chunk * part, part)
        halo_copies.append([
            send(p_send.at[s, span], p_recv.at[s, span],
                 p_ss.at[s, chunk], p_rs.at[s, chunk], side)
            for s, side in ((0, left), (1, right))
        ])

    for copy in loads[2:5]:
        copy.wait()
    scatter(
        obs_cell[...], obs_weight[...], obs_weight[...] * obs_value[...], hot_hi, hot_lo
    )
    sums = lax.dot_general(
        hot_hi[...], hot_lo[...], (((1,), (1,)), ((), ())), preferred_element_type=jnp.float32
    )
    for which in range(2):
        whole = sums[:, which * PIECES * LANES : (which * PIECES + 1) * LANES]
        for i in range(1, PIECES):
            at = (which * PIECES + i) * LANES
            whole = whole + sums[:, at : at + LANES]
        for level in range(levels):
            for block in range(rows // LANES):
                at = (level * (rows // LANES) + block) * 8
                weights[which, level, :, block * LANES : (block + 1) * LANES] = whole[at : at + 8]

    for copy in coeff_copies:
        copy.wait()
    for pair in range(levels // 2):
        for i in range(2):
            level = 2 * pair + i
            halo = halo_tile(c_recv[0, pair], c_recv[1, pair], i)
            f = faces(coeff[level], halo)
            fx_out[0, level], fx_out[1, level], fy_out[0, level], fy_out[1, level] = f

    loads[7].wait()
    for level in range(levels):
        f = (fx_out[0, level], fx_out[1, level], fy_out[0, level], fy_out[1, level])

        def smooth(i, acc):
            span = pl.ds(i * BATCH, BATCH)
            own, halo = diffuse(alpha[span, level], jnp.zeros((BATCH, 8, rows), jnp.float32), *f)
            tail[span, level] = halo
            return acc + jnp.sum(perturb[span, level].astype(jnp.float32) * own, axis=0)

        total[0, level] = lax.fori_loop(
            0, members // BATCH, smooth, jnp.zeros((8, rows), jnp.float32)
        )

    edge = [jnp.zeros((8, rows), jnp.float32)] * levels
    for chunk in range(CHUNKS):
        for copy in halo_copies[chunk]:
            copy.wait()

        def gather(m, acc):
            out = []
            for level in range(levels):
                halo = halo_tile(p_recv[0, m, level // 2], p_recv[1, m, level // 2], level % 2)
                ph_out[m, level] = halo
                out.append(acc[level] + halo * tail[m, level])
            return tuple(out)

        edge = lax.fori_loop(chunk * part, (chunk + 1) * part, gather, tuple(edge))
    for pair in range(levels // 2):
        low, high = pack(edge[2 * pair], edge[2 * pair + 1])
        e_send[0, pair] = low
        e_send[1, pair] = high
    edge_copies = [
        send(e_send.at[s], e_recv.at[s], e_ss.at[s], e_rs.at[s], side)
        for s, side in ((0, right), (1, left))
    ]
    for copy in edge_copies:
        copy.wait()
    for level in range(levels):
        total[0, level] = total[0, level] + halo_tile(
            e_recv[0, level // 2], e_recv[1, level // 2], level % 2
        )
    sums_copies = []
    for r in range(1, n_ens):
        copy = pltpu.make_async_remote_copy(
            src_ref=total.at[0], dst_ref=total.at[r],
            send_sem=t_ss.at[r], recv_sem=t_rs.at[r],
            device_id=(me, lax.rem(ens + r, n_ens)), device_id_type=MESH,
        )
        copy.start()
        sums_copies.append(copy)
    for copy in sums_copies:
        copy.wait()
    increment = total[lax.rem(ens + n_ens, n_ens)]
    for j in range(1, n_ens):
        increment = increment + total[lax.rem(ens - j + n_ens, n_ens)]
    loads[5].wait()
    loads[6].wait()
    state = sigma[...] * static[...] + scale * increment
    adjoint = weights[0] * state - weights[1]
    adj_out[0] = adjoint
    for pair in range(levels // 2):
        low, high = pack(adjoint[2 * pair], adjoint[2 * pair + 1])
        a_send[0, pair] = low
        a_send[1, pair] = high
    adjoint_copies = [
        send(a_send.at[s], a_recv.at[s], a_ss.at[s], a_rs.at[s], side)
        for s, side in ((0, left), (1, right))
    ]
    gs_out[...] = static[...] + sigma[...] * adjoint
    gs_copy = pltpu.make_async_copy(gs_out, gs, gs_sem)
    gs_copy.start()
    for copy in adjoint_copies:
        copy.wait()
    for level in range(levels):
        adj_out[1, level] = halo_tile(a_recv[0, level // 2], a_recv[1, level // 2], level % 2)

    def step(i, carry):
        span = pl.ds(i * BATCH, BATCH)
        for level in range(levels):
            own = perturb[span, level].astype(jnp.float32) * adj_out[0, level]
            halo = ph_out[span, level] * adj_out[1, level]
            own, halo = diffuse(
                own, halo, fx_out[0, level], fx_out[1, level], fy_out[0, level], fy_out[1, level]
            )
            tail[span, level] = alpha[span, level] + scale * own
        pltpu.make_async_copy(tail.at[span], ga.at[span], ga_sem.at[i]).start()
        return carry

    lax.fori_loop(0, members // BATCH, step, 0)
    for i in range(members // BATCH):
        span = pl.ds(i * BATCH, BATCH)
        pltpu.make_async_copy(tail.at[span], ga.at[span], ga_sem.at[i]).wait()
    gs_copy.wait()


def halo_tile(first, second, i):
    top = sublane(first.shape) < 4
    if i == 0:
        return jnp.where(top, first, roll(second, 4, -2))
    return jnp.where(top, roll(first, 4, -2), second)


def per_device(
    alpha, perturb, static_ctl, sigma, class_index, class_kappa, obs_cell, obs_value, obs_weight
):
    n_dom, n_ens = lax.axis_size("dom"), lax.axis_size("ens")
    local, levels, columns, rows = alpha.shape
    assert columns == 8 and levels == 4 and rows == 512
    scale = 1.0 / math.sqrt(local * n_ens - 1)
    groups = obs_cell.shape[0] // LANES
    f32 = jnp.float32
    tile = (levels, columns, rows)
    half = (2, levels // 2, columns, rows)
    hbm = pl.BlockSpec(memory_space=pltpu.HBM)
    dma = pltpu.SemaphoreType.DMA
    return pl.pallas_call(
        functools.partial(exchange, n_dom, n_ens, scale),
        out_shape=(
            jax.ShapeDtypeStruct(alpha.shape, f32),
            jax.ShapeDtypeStruct(tile, f32),
        ),
        in_specs=[hbm] * 9,
        out_specs=(hbm,) * 2,
        scratch_shapes=[
            pltpu.VMEM((2,) + tile, f32),
            pltpu.VMEM(alpha.shape, f32),
            pltpu.VMEM((2,) + tile, f32),
            pltpu.VMEM((2,) + tile, f32),
            pltpu.VMEM(alpha.shape, f32),
            pltpu.VMEM(perturb.shape, perturb.dtype),
            pltpu.VMEM(tile, f32),
            pltpu.SMEM(class_kappa.shape, f32),
            pltpu.VMEM(tile, f32),
            pltpu.VMEM(tile, f32),
            pltpu.VMEM(tile, jnp.int32),
            pltpu.VMEM((groups, LANES), jnp.int32),
            pltpu.VMEM((groups, LANES), f32),
            pltpu.VMEM((groups, LANES), f32),
            pltpu.VMEM(half, f32),
            pltpu.VMEM(half, f32),
            pltpu.VMEM((2, local) + half[1:], f32),
            pltpu.VMEM((2, local) + half[1:], f32),
            pltpu.VMEM(half, f32),
            pltpu.VMEM(half, f32),
            pltpu.VMEM(half, f32),
            pltpu.VMEM(half, f32),
            pltpu.VMEM((n_ens,) + tile, f32),
            pltpu.VMEM((local,) + tile, f32),
            pltpu.VMEM((2,) + tile, f32),
            pltpu.VMEM((LANES, groups * LANES), jnp.bfloat16),
            pltpu.VMEM((2 * PIECES * LANES, groups * LANES), jnp.bfloat16),
            dma((8,)), dma((CHUNKS,)), dma((local // BATCH,)), dma(()),
            dma((2,)), dma((2,)),
            dma((2, CHUNKS)), dma((2, CHUNKS)),
            dma((2,)), dma((2,)),
            dma((2,)), dma((2,)),
            dma((n_ens,)), dma((n_ens,)),
        ],
        compiler_params=pltpu.CompilerParams(
            collective_id=0, has_side_effects=True, vmem_limit_bytes=60 * 2**20
        ),
        name="exchange",
    )(
        class_kappa, alpha, perturb, static_ctl, sigma, class_index,
        obs_cell.reshape(groups, LANES), obs_value.reshape(groups, LANES),
        obs_weight.reshape(groups, LANES),
    )

def solution(mesh):
    return jax.shard_map(
        per_device,
        mesh=mesh,
        in_specs=(
            P("ens", None, "dom", None),
            P("ens", None, "dom", None),
            P(None, "dom", None),
            P(None, "dom", None),
            P(None, "dom", None),
            P(),
            P("dom"),
            P("dom"),
            P("dom"),
        ),
        out_specs=(P("ens", None, "dom", None), P(None, "dom", None)),
        check_vma=False,
    )
```

```python
import functools
import math

import jax
import jax.numpy as jnp
from jax import lax
from jax.experimental import pallas as pl
from jax.experimental.pallas import tpu as pltpu
from jax.sharding import PartitionSpec as P

PASSES = 4
MESH = pl.DeviceIdType.MESH
LANES = 128
PIECES = 3
CHUNKS = 5
BATCH = 2


def sublane(shape):
    return lax.broadcasted_iota(jnp.int32, shape, len(shape) - 2)


def roll(x, shift, axis):
    return pltpu.roll(x, shift, axis % x.ndim)


def toward_right(own, halo):
    last = sublane(own.shape) == 7
    a, b = roll(own, 7, -2), roll(halo, 7, -2)
    return jnp.where(last, b, a), jnp.where(last, a, b)


def toward_left(own, halo):
    first = sublane(own.shape) == 0
    a, b = roll(own, 1, -2), roll(halo, 1, -2)
    return jnp.where(first, b, a), jnp.where(first, a, b)


def pack(a, b):
    top = sublane(a.shape) < 4
    return jnp.where(top, a, roll(b, 4, -2)), jnp.where(top, roll(a, 4, -2), b)


def faces(own, halo):
    right_own, right_halo = toward_right(own, halo)
    rows = own.shape[-1]
    inside = lax.broadcasted_iota(jnp.int32, own.shape, own.ndim - 1) < rows - 1
    zero = jnp.zeros_like(own)
    fx_own = 0.5 * (own + right_own)
    fx_halo = jnp.where(sublane(own.shape) == 3, zero, 0.5 * (halo + right_halo))
    fy_own = jnp.where(inside, 0.5 * (own + roll(own, rows - 1, -1)), zero)
    fy_halo = jnp.where(inside, 0.5 * (halo + roll(halo, rows - 1, -1)), zero)
    return fx_own, fx_halo, fy_own, fy_halo


def diffuse(own, halo, fx_own, fx_halo, fy_own, fy_halo):
    rows = own.shape[-1]
    for _ in range(PASSES):
        right_own, right_halo = toward_right(own, halo)
        flux_own = fx_own * (right_own - own)
        flux_halo = fx_halo * (right_halo - halo)
        left_own, left_halo = toward_left(flux_own, flux_halo)
        up_own = fy_own * (roll(own, rows - 1, -1) - own)
        up_halo = fy_halo * (roll(halo, rows - 1, -1) - halo)
        own = own + (flux_own - left_own) + (up_own - roll(up_own, 1, -1))
        halo = halo + (flux_halo - left_halo) + (up_halo - roll(up_halo, 1, -1))
    return own, halo


def split3(x):
    out = []
    for _ in range(PIECES):
        piece = x.astype(jnp.bfloat16)
        out.append(piece.astype(jnp.float32))
        x = x - out[-1]
    return out


def scatter(cell, weight, product, hot_hi, hot_lo):
    groups = cell.shape[0]
    spot = lax.broadcasted_iota(jnp.int32, (LANES, LANES), 0)
    for g in range(groups):
        c = cell[g : g + 1, :]
        hi = (c // 4096) * 32 + ((c // 128) % 4) * 8 + (c // 512) % 8
        lo = c % 128
        lanes = slice(g * LANES, (g + 1) * LANES)
        hot_hi[:, lanes] = (spot == hi).astype(jnp.float32).astype(jnp.bfloat16)
        here = spot == lo
        values = split3(weight[g : g + 1, :]) + split3(product[g : g + 1, :])
        for i, value in enumerate(values):
            hot_lo[i * LANES : (i + 1) * LANES, lanes] = jnp.where(here, value, 0.0).astype(
                jnp.bfloat16
            )


def exchange(
    n_dom, n_ens, scale,
    kappa_in, alpha_in, perturb_in, static_in, sigma_in, index_in, cell_in, value_in, weight_in,
    ga, gs,
    adj_out, ph_out, fx_out, fy_out, alpha, perturb, gs_out, kappa, static, sigma, index, obs_cell, obs_value, obs_weight,
    c_send, c_recv, p_send, p_recv, e_send, e_recv, a_send, a_recv, total,
    tail, weights, hot_hi, hot_lo,
    in_sem, pin_sem, ga_sem, gs_sem, c_ss, c_rs, p_ss, p_rs, e_ss, e_rs, a_ss, a_rs, t_ss, t_rs,
):
    me, ens = lax.axis_index("dom"), lax.axis_index("ens")
    right, left = lax.rem(me + 1, n_dom), lax.rem(me + n_dom - 1, n_dom)
    members, levels = alpha.shape[0], alpha.shape[1]
    rows = alpha.shape[3]

    part = members // CHUNKS
    loads = []
    for i, (src, dst) in enumerate((
        (kappa_in, kappa), (index_in, index), (cell_in, obs_cell), (value_in, obs_value),
        (weight_in, obs_weight), (static_in, static), (sigma_in, sigma), (alpha_in, alpha),
    )):
        loads.append(pltpu.make_async_copy(src, dst, in_sem.at[i]))
    perturb_loads = [
        pltpu.make_async_copy(
            perturb_in.at[pl.ds(c * part, part)], perturb.at[pl.ds(c * part, part)], pin_sem.at[c]
        )
        for c in range(CHUNKS)
    ]
    for copy in loads[:2] + perturb_loads + loads[2:]:
        copy.start()

    barrier = pltpu.get_barrier_semaphore()
    for side in (left, right):
        pl.semaphore_signal(barrier, inc=1, device_id=(side, ens), device_id_type=MESH)
    for r in range(1, n_ens):
        pl.semaphore_signal(
            barrier, inc=1, device_id=(me, lax.rem(ens + r, n_ens)), device_id_type=MESH
        )

    def send(src, dst, ss, rs, side):
        copy = pltpu.make_async_remote_copy(
            src_ref=src, dst_ref=dst, send_sem=ss, recv_sem=rs,
            device_id=(side, ens), device_id_type=MESH,
        )
        copy.start()
        return copy

    loads[0].wait()
    loads[1].wait()
    cls = index[...]
    coeff = jnp.zeros(cls.shape, jnp.float32)
    for number in range(kappa.shape[0]):
        coeff = jnp.where(cls == number, kappa[number], coeff)
    for pair in range(levels // 2):
        low, high = pack(coeff[2 * pair], coeff[2 * pair + 1])
        c_send[0, pair] = low
        c_send[1, pair] = high
    pl.semaphore_wait(barrier, 2 + n_ens - 1)
    coeff_copies = [
        send(c_send.at[s], c_recv.at[s], c_ss.at[s], c_rs.at[s], side)
        for s, side in ((0, left), (1, right))
    ]
    halo_copies = []
    for chunk in range(CHUNKS):
        perturb_loads[chunk].wait()

        def fill(m, carry):
            for pair in range(levels // 2):
                a = perturb[m, 2 * pair].astype(jnp.float32)
                b = perturb[m, 2 * pair + 1].astype(jnp.float32)
                low, high = pack(a, b)
                p_send[0, m, pair] = low
                p_send[1, m, pair] = high
            return carry

        lax.fori_loop(chunk * part, (chunk + 1) * part, fill, 0)
        span = pl.ds(chunk * part, part)
        halo_copies.append([
            send(p_send.at[s, span], p_recv.at[s, span],
                 p_ss.at[s, chunk], p_rs.at[s, chunk], side)
            for s, side in ((0, left), (1, right))
        ])

    for copy in loads[2:5]:
        copy.wait()
    scatter(
        obs_cell[...], obs_weight[...], obs_weight[...] * obs_value[...], hot_hi, hot_lo
    )
    sums = lax.dot_general(
        hot_hi[...], hot_lo[...], (((1,), (1,)), ((), ())), preferred_element_type=jnp.float32
    )
    for which in range(2):
        whole = sums[:, which * PIECES * LANES : (which * PIECES + 1) * LANES]
        for i in range(1, PIECES):
            at = (which * PIECES + i) * LANES
            whole = whole + sums[:, at : at + LANES]
        for level in range(levels):
            for block in range(rows // LANES):
                at = (level * (rows // LANES) + block) * 8
                weights[which, level, :, block * LANES : (block + 1) * LANES] = whole[at : at + 8]

    for copy in coeff_copies:
        copy.wait()
    for pair in range(levels // 2):
        for i in range(2):
            level = 2 * pair + i
            halo = halo_tile(c_recv[0, pair], c_recv[1, pair], i)
            f = faces(coeff[level], halo)
            fx_out[0, level], fx_out[1, level], fy_out[0, level], fy_out[1, level] = f

    loads[7].wait()
    def smooth(i, acc):
        span = pl.ds(i * BATCH, BATCH)
        for level in range(levels):
            own, halo = diffuse(
                alpha[span, level], jnp.zeros((BATCH, 8, rows), jnp.float32),
                fx_out[0, level], fx_out[1, level], fy_out[0, level], fy_out[1, level],
            )
            tail[span, level] = halo
            total[0, level] = total[0, level] + jnp.sum(
                perturb[span, level].astype(jnp.float32) * own, axis=0
            )
        return acc

    total[0] = jnp.zeros(total.shape[1:], jnp.float32)
    lax.fori_loop(0, members // BATCH, smooth, 0)

    edge = [jnp.zeros((8, rows), jnp.float32)] * levels
    for chunk in range(CHUNKS):
        for copy in halo_copies[chunk]:
            copy.wait()

        def gather(m, acc):
            out = []
            for level in range(levels):
                halo = halo_tile(p_recv[0, m, level // 2], p_recv[1, m, level // 2], level % 2)
                ph_out[m, level] = halo
                out.append(acc[level] + halo * tail[m, level])
            return tuple(out)

        edge = lax.fori_loop(chunk * part, (chunk + 1) * part, gather, tuple(edge))
    for pair in range(levels // 2):
        low, high = pack(edge[2 * pair], edge[2 * pair + 1])
        e_send[0, pair] = low
        e_send[1, pair] = high
    edge_copies = [
        send(e_send.at[s], e_recv.at[s], e_ss.at[s], e_rs.at[s], side)
        for s, side in ((0, right), (1, left))
    ]
    for copy in edge_copies:
        copy.wait()
    for level in range(levels):
        total[0, level] = total[0, level] + halo_tile(
            e_recv[0, level // 2], e_recv[1, level // 2], level % 2
        )
    sums_copies = []
    for r in range(1, n_ens):
        copy = pltpu.make_async_remote_copy(
            src_ref=total.at[0], dst_ref=total.at[r],
            send_sem=t_ss.at[r], recv_sem=t_rs.at[r],
            device_id=(me, lax.rem(ens + r, n_ens)), device_id_type=MESH,
        )
        copy.start()
        sums_copies.append(copy)
    for copy in sums_copies:
        copy.wait()
    increment = total[lax.rem(ens + n_ens, n_ens)]
    for j in range(1, n_ens):
        increment = increment + total[lax.rem(ens - j + n_ens, n_ens)]
    loads[5].wait()
    loads[6].wait()
    state = sigma[...] * static[...] + scale * increment
    adjoint = weights[0] * state - weights[1]
    adj_out[0] = adjoint
    for pair in range(levels // 2):
        low, high = pack(adjoint[2 * pair], adjoint[2 * pair + 1])
        a_send[0, pair] = low
        a_send[1, pair] = high
    adjoint_copies = [
        send(a_send.at[s], a_recv.at[s], a_ss.at[s], a_rs.at[s], side)
        for s, side in ((0, left), (1, right))
    ]
    gs_out[...] = static[...] + sigma[...] * adjoint
    gs_copy = pltpu.make_async_copy(gs_out, gs, gs_sem)
    gs_copy.start()
    for copy in adjoint_copies:
        copy.wait()
    for level in range(levels):
        adj_out[1, level] = halo_tile(a_recv[0, level // 2], a_recv[1, level // 2], level % 2)

    def step(i, carry):
        span = pl.ds(i * BATCH, BATCH)
        for level in range(levels):
            own = perturb[span, level].astype(jnp.float32) * adj_out[0, level]
            halo = ph_out[span, level] * adj_out[1, level]
            own, halo = diffuse(
                own, halo, fx_out[0, level], fx_out[1, level], fy_out[0, level], fy_out[1, level]
            )
            tail[span, level] = alpha[span, level] + scale * own
        pltpu.make_async_copy(tail.at[span], ga.at[span], ga_sem.at[i]).start()
        return carry

    lax.fori_loop(0, members // BATCH, step, 0)
    for i in range(members // BATCH):
        span = pl.ds(i * BATCH, BATCH)
        pltpu.make_async_copy(tail.at[span], ga.at[span], ga_sem.at[i]).wait()
    gs_copy.wait()


def halo_tile(first, second, i):
    top = sublane(first.shape) < 4
    if i == 0:
        return jnp.where(top, first, roll(second, 4, -2))
    return jnp.where(top, roll(first, 4, -2), second)


def per_device(
    alpha, perturb, static_ctl, sigma, class_index, class_kappa, obs_cell, obs_value, obs_weight
):
    n_dom, n_ens = lax.axis_size("dom"), lax.axis_size("ens")
    local, levels, columns, rows = alpha.shape
    assert columns == 8 and levels == 4 and rows == 512
    scale = 1.0 / math.sqrt(local * n_ens - 1)
    groups = obs_cell.shape[0] // LANES
    f32 = jnp.float32
    tile = (levels, columns, rows)
    half = (2, levels // 2, columns, rows)
    hbm = pl.BlockSpec(memory_space=pltpu.HBM)
    dma = pltpu.SemaphoreType.DMA
    return pl.pallas_call(
        functools.partial(exchange, n_dom, n_ens, scale),
        out_shape=(
            jax.ShapeDtypeStruct(alpha.shape, f32),
            jax.ShapeDtypeStruct(tile, f32),
        ),
        in_specs=[hbm] * 9,
        out_specs=(hbm,) * 2,
        scratch_shapes=[
            pltpu.VMEM((2,) + tile, f32),
            pltpu.VMEM(alpha.shape, f32),
            pltpu.VMEM((2,) + tile, f32),
            pltpu.VMEM((2,) + tile, f32),
            pltpu.VMEM(alpha.shape, f32),
            pltpu.VMEM(perturb.shape, perturb.dtype),
            pltpu.VMEM(tile, f32),
            pltpu.SMEM(class_kappa.shape, f32),
            pltpu.VMEM(tile, f32),
            pltpu.VMEM(tile, f32),
            pltpu.VMEM(tile, jnp.int32),
            pltpu.VMEM((groups, LANES), jnp.int32),
            pltpu.VMEM((groups, LANES), f32),
            pltpu.VMEM((groups, LANES), f32),
            pltpu.VMEM(half, f32),
            pltpu.VMEM(half, f32),
            pltpu.VMEM((2, local) + half[1:], f32),
            pltpu.VMEM((2, local) + half[1:], f32),
            pltpu.VMEM(half, f32),
            pltpu.VMEM(half, f32),
            pltpu.VMEM(half, f32),
            pltpu.VMEM(half, f32),
            pltpu.VMEM((n_ens,) + tile, f32),
            pltpu.VMEM((local,) + tile, f32),
            pltpu.VMEM((2,) + tile, f32),
            pltpu.VMEM((LANES, groups * LANES), jnp.bfloat16),
            pltpu.VMEM((2 * PIECES * LANES, groups * LANES), jnp.bfloat16),
            dma((8,)), dma((CHUNKS,)), dma((local // BATCH,)), dma(()),
            dma((2,)), dma((2,)),
            dma((2, CHUNKS)), dma((2, CHUNKS)),
            dma((2,)), dma((2,)),
            dma((2,)), dma((2,)),
            dma((n_ens,)), dma((n_ens,)),
        ],
        compiler_params=pltpu.CompilerParams(
            collective_id=0, has_side_effects=True, vmem_limit_bytes=60 * 2**20
        ),
        name="exchange",
    )(
        class_kappa, alpha, perturb, static_ctl, sigma, class_index,
        obs_cell.reshape(groups, LANES), obs_value.reshape(groups, LANES),
        obs_weight.reshape(groups, LANES),
    )

def solution(mesh):
    return jax.shard_map(
        per_device,
        mesh=mesh,
        in_specs=(
            P("ens", None, "dom", None),
            P("ens", None, "dom", None),
            P(None, "dom", None),
            P(None, "dom", None),
            P(None, "dom", None),
            P(),
            P("dom"),
            P("dom"),
            P("dom"),
        ),
        out_specs=(P("ens", None, "dom", None), P(None, "dom", None)),
        check_vma=False,
    )
```

```python
import functools
import math

import jax
import jax.numpy as jnp
from jax import lax
from jax.experimental import pallas as pl
from jax.experimental.pallas import tpu as pltpu
from jax.sharding import PartitionSpec as P

PASSES = 4
MESH = pl.DeviceIdType.MESH
LANES = 128
PIECES = 3
CHUNKS = 5
BATCH = 2


def sublane(shape):
    return lax.broadcasted_iota(jnp.int32, shape, len(shape) - 2)


def roll(x, shift, axis):
    return pltpu.roll(x, shift, axis % x.ndim)


def toward_right(own, halo):
    last = sublane(own.shape) == 7
    a, b = roll(own, 7, -2), roll(halo, 7, -2)
    return jnp.where(last, b, a), jnp.where(last, a, b)


def toward_left(own, halo):
    first = sublane(own.shape) == 0
    a, b = roll(own, 1, -2), roll(halo, 1, -2)
    return jnp.where(first, b, a), jnp.where(first, a, b)


def pack(a, b):
    top = sublane(a.shape) < 4
    return jnp.where(top, a, roll(b, 4, -2)), jnp.where(top, roll(a, 4, -2), b)


def faces(own, halo):
    right_own, right_halo = toward_right(own, halo)
    rows = own.shape[-1]
    inside = lax.broadcasted_iota(jnp.int32, own.shape, own.ndim - 1) < rows - 1
    zero = jnp.zeros_like(own)
    fx_own = 0.5 * (own + right_own)
    fx_halo = jnp.where(sublane(own.shape) == 3, zero, 0.5 * (halo + right_halo))
    fy_own = jnp.where(inside, 0.5 * (own + roll(own, rows - 1, -1)), zero)
    fy_halo = jnp.where(inside, 0.5 * (halo + roll(halo, rows - 1, -1)), zero)
    return fx_own, fx_halo, fy_own, fy_halo


def diffuse(own, halo, fx_own, fx_halo, fy_own, fy_halo):
    rows = own.shape[-1]
    for _ in range(PASSES):
        right_own, right_halo = toward_right(own, halo)
        flux_own = fx_own * (right_own - own)
        flux_halo = fx_halo * (right_halo - halo)
        left_own, left_halo = toward_left(flux_own, flux_halo)
        up_own = fy_own * (roll(own, rows - 1, -1) - own)
        up_halo = fy_halo * (roll(halo, rows - 1, -1) - halo)
        own = own + (flux_own - left_own) + (up_own - roll(up_own, 1, -1))
        halo = halo + (flux_halo - left_halo) + (up_halo - roll(up_halo, 1, -1))
    return own, halo


def split3(x):
    out = []
    for _ in range(PIECES):
        piece = x.astype(jnp.bfloat16)
        out.append(piece.astype(jnp.float32))
        x = x - out[-1]
    return out


def scatter(cell, weight, product, hot_hi, hot_lo):
    groups = cell.shape[0]
    spot = lax.broadcasted_iota(jnp.int32, (LANES, LANES), 0)
    for g in range(groups):
        c = cell[g : g + 1, :]
        hi = (c // 4096) * 32 + ((c // 128) % 4) * 8 + (c // 512) % 8
        lo = c % 128
        lanes = slice(g * LANES, (g + 1) * LANES)
        hot_hi[:, lanes] = (spot == hi).astype(jnp.float32).astype(jnp.bfloat16)
        here = spot == lo
        values = split3(weight[g : g + 1, :]) + split3(product[g : g + 1, :])
        for i, value in enumerate(values):
            hot_lo[i * LANES : (i + 1) * LANES, lanes] = jnp.where(here, value, 0.0).astype(
                jnp.bfloat16
            )


def exchange(
    n_dom, n_ens, scale,
    kappa_in, alpha_in, perturb_in, static_in, sigma_in, index_in, cell_in, value_in, weight_in,
    ga, gs,
    adj_out, ph_out, fx_out, fy_out, alpha, perturb, gs_out, kappa, static, sigma, index, obs_cell, obs_value, obs_weight,
    c_send, c_recv, p_send, p_recv, e_send, e_recv, a_send, a_recv, total,
    tail, weights, hot_hi, hot_lo,
    in_sem, pin_sem, ga_sem, gs_sem, c_ss, c_rs, p_ss, p_rs, e_ss, e_rs, a_ss, a_rs, t_ss, t_rs,
):
    me, ens = lax.axis_index("dom"), lax.axis_index("ens")
    right, left = lax.rem(me + 1, n_dom), lax.rem(me + n_dom - 1, n_dom)
    members, levels = alpha.shape[0], alpha.shape[1]
    rows = alpha.shape[3]

    part = members // CHUNKS
    loads = []
    for i, (src, dst) in enumerate((
        (kappa_in, kappa), (index_in, index), (cell_in, obs_cell), (value_in, obs_value),
        (weight_in, obs_weight), (static_in, static), (sigma_in, sigma), (alpha_in, alpha),
    )):
        loads.append(pltpu.make_async_copy(src, dst, in_sem.at[i]))
    perturb_loads = [
        pltpu.make_async_copy(
            perturb_in.at[pl.ds(c * part, part)], perturb.at[pl.ds(c * part, part)], pin_sem.at[c]
        )
        for c in range(CHUNKS)
    ]
    for copy in perturb_loads[:1] + loads[:2] + perturb_loads[1:] + loads[2:]:
        copy.start()

    barrier = pltpu.get_barrier_semaphore()
    for side in (left, right):
        pl.semaphore_signal(barrier, inc=1, device_id=(side, ens), device_id_type=MESH)
    for r in range(1, n_ens):
        pl.semaphore_signal(
            barrier, inc=1, device_id=(me, lax.rem(ens + r, n_ens)), device_id_type=MESH
        )

    def send(src, dst, ss, rs, side):
        copy = pltpu.make_async_remote_copy(
            src_ref=src, dst_ref=dst, send_sem=ss, recv_sem=rs,
            device_id=(side, ens), device_id_type=MESH,
        )
        copy.start()
        return copy

    halo_copies = []

    def push(chunk):
        perturb_loads[chunk].wait()

        def fill(m, carry):
            for pair in range(levels // 2):
                a = perturb[m, 2 * pair].astype(jnp.float32)
                b = perturb[m, 2 * pair + 1].astype(jnp.float32)
                low, high = pack(a, b)
                p_send[0, m, pair] = low
                p_send[1, m, pair] = high
            return carry

        lax.fori_loop(chunk * part, (chunk + 1) * part, fill, 0, unroll=True)
        span = pl.ds(chunk * part, part)
        if chunk == 0:
            pl.semaphore_wait(barrier, 2 + n_ens - 1)
        halo_copies.append([
            send(p_send.at[s, span], p_recv.at[s, span],
                 p_ss.at[s, chunk], p_rs.at[s, chunk], side)
            for s, side in ((0, left), (1, right))
        ])

    push(0)
    loads[0].wait()
    loads[1].wait()
    cls = index[...]
    coeff = jnp.zeros(cls.shape, jnp.float32)
    for number in range(kappa.shape[0]):
        coeff = jnp.where(cls == number, kappa[number], coeff)
    for pair in range(levels // 2):
        low, high = pack(coeff[2 * pair], coeff[2 * pair + 1])
        c_send[0, pair] = low
        c_send[1, pair] = high
    coeff_copies = [
        send(c_send.at[s], c_recv.at[s], c_ss.at[s], c_rs.at[s], side)
        for s, side in ((0, left), (1, right))
    ]
    for chunk in range(1, CHUNKS):
        push(chunk)

    for copy in loads[2:5]:
        copy.wait()
    scatter(
        obs_cell[...], obs_weight[...], obs_weight[...] * obs_value[...], hot_hi, hot_lo
    )
    sums = lax.dot_general(
        hot_hi[...], hot_lo[...], (((1,), (1,)), ((), ())), preferred_element_type=jnp.float32
    )
    for which in range(2):
        whole = sums[:, which * PIECES * LANES : (which * PIECES + 1) * LANES]
        for i in range(1, PIECES):
            at = (which * PIECES + i) * LANES
            whole = whole + sums[:, at : at + LANES]
        for level in range(levels):
            for block in range(rows // LANES):
                at = (level * (rows // LANES) + block) * 8
                weights[which, level, :, block * LANES : (block + 1) * LANES] = whole[at : at + 8]

    for copy in coeff_copies:
        copy.wait()
    for pair in range(levels // 2):
        for i in range(2):
            level = 2 * pair + i
            halo = halo_tile(c_recv[0, pair], c_recv[1, pair], i)
            f = faces(coeff[level], halo)
            fx_out[0, level], fx_out[1, level], fy_out[0, level], fy_out[1, level] = f

    loads[7].wait()
    def smooth(i, acc):
        span = pl.ds(i * BATCH, BATCH)
        for level in range(levels):
            own, halo = diffuse(
                alpha[span, level], jnp.zeros((BATCH, 8, rows), jnp.float32),
                fx_out[0, level], fx_out[1, level], fy_out[0, level], fy_out[1, level],
            )
            tail[span, level] = halo
            total[0, level] = total[0, level] + jnp.sum(
                perturb[span, level].astype(jnp.float32) * own, axis=0
            )
        return acc

    total[0] = jnp.zeros(total.shape[1:], jnp.float32)
    lax.fori_loop(0, members // BATCH, smooth, 0)

    edge = [jnp.zeros((8, rows), jnp.float32)] * levels
    for chunk in range(CHUNKS):
        for copy in halo_copies[chunk]:
            copy.wait()

        def gather(m, acc):
            out = []
            for level in range(levels):
                halo = halo_tile(p_recv[0, m, level // 2], p_recv[1, m, level // 2], level % 2)
                ph_out[m, level] = halo
                out.append(acc[level] + halo * tail[m, level])
            return tuple(out)

        edge = lax.fori_loop(chunk * part, (chunk + 1) * part, gather, tuple(edge), unroll=True)
    for pair in range(levels // 2):
        low, high = pack(edge[2 * pair], edge[2 * pair + 1])
        e_send[0, pair] = low
        e_send[1, pair] = high
    edge_copies = [
        send(e_send.at[s], e_recv.at[s], e_ss.at[s], e_rs.at[s], side)
        for s, side in ((0, right), (1, left))
    ]
    for copy in edge_copies:
        copy.wait()
    for level in range(levels):
        total[0, level] = total[0, level] + halo_tile(
            e_recv[0, level // 2], e_recv[1, level // 2], level % 2
        )
    sums_copies = []
    for r in range(1, n_ens):
        copy = pltpu.make_async_remote_copy(
            src_ref=total.at[0], dst_ref=total.at[r],
            send_sem=t_ss.at[r], recv_sem=t_rs.at[r],
            device_id=(me, lax.rem(ens + r, n_ens)), device_id_type=MESH,
        )
        copy.start()
        sums_copies.append(copy)
    for copy in sums_copies:
        copy.wait()
    increment = total[lax.rem(ens + n_ens, n_ens)]
    for j in range(1, n_ens):
        increment = increment + total[lax.rem(ens - j + n_ens, n_ens)]
    loads[5].wait()
    loads[6].wait()
    state = sigma[...] * static[...] + scale * increment
    adjoint = weights[0] * state - weights[1]
    adj_out[0] = adjoint
    for pair in range(levels // 2):
        low, high = pack(adjoint[2 * pair], adjoint[2 * pair + 1])
        a_send[0, pair] = low
        a_send[1, pair] = high
    adjoint_copies = [
        send(a_send.at[s], a_recv.at[s], a_ss.at[s], a_rs.at[s], side)
        for s, side in ((0, left), (1, right))
    ]
    gs_out[...] = static[...] + sigma[...] * adjoint
    gs_copy = pltpu.make_async_copy(gs_out, gs, gs_sem)
    gs_copy.start()
    for copy in adjoint_copies:
        copy.wait()
    for level in range(levels):
        adj_out[1, level] = halo_tile(a_recv[0, level // 2], a_recv[1, level // 2], level % 2)

    def step(i, carry):
        span = pl.ds(i * BATCH, BATCH)
        for level in range(levels):
            own = perturb[span, level].astype(jnp.float32) * adj_out[0, level]
            halo = ph_out[span, level] * adj_out[1, level]
            own, halo = diffuse(
                own, halo, fx_out[0, level], fx_out[1, level], fy_out[0, level], fy_out[1, level]
            )
            tail[span, level] = alpha[span, level] + scale * own
        pltpu.make_async_copy(tail.at[span], ga.at[span], ga_sem.at[i]).start()
        return carry

    lax.fori_loop(0, members // BATCH, step, 0)
    for i in range(members // BATCH):
        span = pl.ds(i * BATCH, BATCH)
        pltpu.make_async_copy(tail.at[span], ga.at[span], ga_sem.at[i]).wait()
    gs_copy.wait()


def halo_tile(first, second, i):
    top = sublane(first.shape) < 4
    if i == 0:
        return jnp.where(top, first, roll(second, 4, -2))
    return jnp.where(top, roll(first, 4, -2), second)


def per_device(
    alpha, perturb, static_ctl, sigma, class_index, class_kappa, obs_cell, obs_value, obs_weight
):
    n_dom, n_ens = lax.axis_size("dom"), lax.axis_size("ens")
    local, levels, columns, rows = alpha.shape
    assert columns == 8 and levels == 4 and rows == 512
    scale = 1.0 / math.sqrt(local * n_ens - 1)
    groups = obs_cell.shape[0] // LANES
    f32 = jnp.float32
    tile = (levels, columns, rows)
    half = (2, levels // 2, columns, rows)
    hbm = pl.BlockSpec(memory_space=pltpu.HBM)
    dma = pltpu.SemaphoreType.DMA
    return pl.pallas_call(
        functools.partial(exchange, n_dom, n_ens, scale),
        out_shape=(
            jax.ShapeDtypeStruct(alpha.shape, f32),
            jax.ShapeDtypeStruct(tile, f32),
        ),
        in_specs=[hbm] * 9,
        out_specs=(hbm,) * 2,
        scratch_shapes=[
            pltpu.VMEM((2,) + tile, f32),
            pltpu.VMEM(alpha.shape, f32),
            pltpu.VMEM((2,) + tile, f32),
            pltpu.VMEM((2,) + tile, f32),
            pltpu.VMEM(alpha.shape, f32),
            pltpu.VMEM(perturb.shape, perturb.dtype),
            pltpu.VMEM(tile, f32),
            pltpu.SMEM(class_kappa.shape, f32),
            pltpu.VMEM(tile, f32),
            pltpu.VMEM(tile, f32),
            pltpu.VMEM(tile, jnp.int32),
            pltpu.VMEM((groups, LANES), jnp.int32),
            pltpu.VMEM((groups, LANES), f32),
            pltpu.VMEM((groups, LANES), f32),
            pltpu.VMEM(half, f32),
            pltpu.VMEM(half, f32),
            pltpu.VMEM((2, local) + half[1:], f32),
            pltpu.VMEM((2, local) + half[1:], f32),
            pltpu.VMEM(half, f32),
            pltpu.VMEM(half, f32),
            pltpu.VMEM(half, f32),
            pltpu.VMEM(half, f32),
            pltpu.VMEM((n_ens,) + tile, f32),
            pltpu.VMEM((local,) + tile, f32),
            pltpu.VMEM((2,) + tile, f32),
            pltpu.VMEM((LANES, groups * LANES), jnp.bfloat16),
            pltpu.VMEM((2 * PIECES * LANES, groups * LANES), jnp.bfloat16),
            dma((8,)), dma((CHUNKS,)), dma((local // BATCH,)), dma(()),
            dma((2,)), dma((2,)),
            dma((2, CHUNKS)), dma((2, CHUNKS)),
            dma((2,)), dma((2,)),
            dma((2,)), dma((2,)),
            dma((n_ens,)), dma((n_ens,)),
        ],
        compiler_params=pltpu.CompilerParams(
            collective_id=0, has_side_effects=True, vmem_limit_bytes=60 * 2**20
        ),
        name="exchange",
    )(
        class_kappa, alpha, perturb, static_ctl, sigma, class_index,
        obs_cell.reshape(groups, LANES), obs_value.reshape(groups, LANES),
        obs_weight.reshape(groups, LANES),
    )

def solution(mesh):
    return jax.shard_map(
        per_device,
        mesh=mesh,
        in_specs=(
            P("ens", None, "dom", None),
            P("ens", None, "dom", None),
            P(None, "dom", None),
            P(None, "dom", None),
            P(None, "dom", None),
            P(),
            P("dom"),
            P("dom"),
            P("dom"),
        ),
        out_specs=(P("ens", None, "dom", None), P(None, "dom", None)),
        check_vma=False,
    )
```
